32 devices in a mesh: rows: 8 (over z, y), cols: 4 (over x, core).
Axes of the slice: x: 2, y: 2, z: 4, core: 2. Of those that a mesh axis runs over, the one named last changes fastest.
Arguments:
- hblocks: float32 [64, 24, 128, 128], P('rows'), may hold values from -0.0546875 to 0.0546875
- col_index: int32 [64, 24], P('rows'), may hold values from 0 to 63, as said below
- right_side: float32 [64, 64, 128], P('rows', 'cols'), may hold values from -12 to 12
- center: float32 [1], replicated, may hold values from -0.5 to 0.5
- shifts: float32 [8], replicated, may hold values from 0.05 to 2
- filter_weights: float32 [8], replicated, may hold values from 0.03 to 0.3
Outputs:
- filtered: float32 [64, 64, 128], P('rows', 'cols')
- gram_matrix: float32 [64, 64], P(None, 'cols')
- ritz_matrix: float32 [64, 64], P(None, 'cols')
The draws below stay inside these ranges and needn't reach their ends.
Inputs may be any that keep to these rules, and one draw needn't show every extreme that they name: `col_index`: block rows are held 8 to a device of rows, in order. In block row i the first 8 column indices are the 8 block rows of the device that holds i, each once. Every other column index of a block row lies on another device of rows; for each pair of distinct devices, the block rows of the one that are named by the block rows of the other are exactly 2 distinct ones.
All inputs are finite; a program needn't handle non-finite values.
Results may differ from the reference program's by a relative error of at most 0.0001.
Values sent between devices are 32-bit elements; how exact they have to be, the bound alone decides.
A program may use at most 64 MiB of HBM per device.

```python
import math
import jax
import jax.numpy as jnp
from jax import lax

BLK = 128
NBLK = 24
NVEC = 64
POLES = 8
BR_DEV = 8
CAP = 2
ITERS = 2
NB = 64
N_ROWS = 8


def build_pattern(key):
    list_keys = jax.random.split(jax.random.fold_in(key, 7), N_ROWS * N_ROWS)
    shuffled = jax.vmap(lambda one_key: jax.random.permutation(one_key, BR_DEV))(list_keys)
    chosen = shuffled[:, :CAP].reshape(N_ROWS, N_ROWS, CAP).astype(jnp.int32)
    slot_total = (N_ROWS - 1) * CAP
    far_total = BR_DEV * (NBLK - BR_DEV)

    def one_device(device, device_key):
        extra_slots = jax.random.randint(jax.random.fold_in(device_key, 1), (far_total,), 0, slot_total, dtype=jnp.int32)
        counter = jnp.arange(far_total, dtype=jnp.int32)
        assigned = jnp.where(counter < slot_total, counter, extra_slots)
        assigned = jax.random.permutation(jax.random.fold_in(device_key, 2), assigned)
        owner_dev = assigned // CAP
        owner_dev = owner_dev + (owner_dev >= device).astype(jnp.int32)
        far_cols = owner_dev * BR_DEV + chosen[owner_dev, device, assigned % CAP]
        row_keys = jax.random.split(jax.random.fold_in(device_key, 3), BR_DEV)
        near_cols = jax.vmap(lambda one_key: jax.random.permutation(one_key, BR_DEV))(row_keys) + device * BR_DEV
        return jnp.concatenate([near_cols.astype(jnp.int32), far_cols.reshape(BR_DEV, NBLK - BR_DEV).astype(jnp.int32)], axis=1)
    device_keys = jax.random.split(jax.random.fold_in(key, 11), N_ROWS)
    columns = jax.vmap(one_device)(jnp.arange(N_ROWS, dtype=jnp.int32), device_keys)
    return columns.reshape(NB, NBLK)


def draw_col_index(key, part):
    return build_pattern(key)


def draw_right_side(key, part):
    position = jnp.arange(NB, dtype=jnp.float32)
    row_ramp = 1.0 + 2.0 * position / max(NB - 1, 1)
    row_rough = jnp.exp(jnp.log(2.0) * jax.random.uniform(jax.random.fold_in(key, 1), (NB, 1, 1)))
    col_rough = jnp.exp(jnp.log(2.0) * jax.random.uniform(jax.random.fold_in(key, 2), (1, NVEC, 1)))
    values = jax.random.normal(jax.random.fold_in(key, 3), (NB, NVEC, BLK))
    values = jnp.clip(values, -4.0, 4.0)
    return (values * row_ramp[:, None, None] * row_rough * col_rough / 4.0).astype(jnp.float32)


def block_levels(own_key, dims, cuts, smallest, top_value):
    def one(dim, blocks):
        heights = jax.random.uniform(jax.random.fold_in(jax.random.fold_in(own_key, 6), dim), (blocks,), jnp.float32, smallest / len(cuts), top_value / len(cuts))
        return jnp.repeat(jnp.exp(heights), dims[dim] // blocks).reshape((-1,) + (1,) * (len(dims) - dim - 1))

    loudness = one(*cuts[0])
    for cut in cuts[1:]:
        loudness = loudness * one(*cut)
    return loudness


def normal_values(rng, dims, spread, most, pieces=(), kind=jnp.bfloat16):
    values = jax.random.normal(rng, dims, jnp.float32) * spread
    if len(pieces) > 0:
        values = block_levels(rng, dims, pieces, -0.22, 0.18) * values
    return jnp.clip(values, min=-most, max=most).astype(kind)


def setup_inputs(seed: int = 0) -> dict:
    splits = jax.random.split(jax.random.key(seed), 7)
    return {
        "hblocks": normal_values(splits[0], (NB, NBLK, BLK, BLK), (4 * NBLK * BLK) ** -0.5, 0.0546875, ((0, 8),), jnp.float32),
        "col_index": draw_col_index(jax.random.fold_in(splits[6], 71), 0),
        "right_side": draw_right_side(jax.random.fold_in(splits[6], 71), 0),
        "center": jnp.clip(jax.random.uniform(splits[3], (1,), jnp.float32, -0.5, 0.5), -0.5, 0.5),
        "shifts": jnp.clip(jnp.exp(jax.random.uniform(splits[4], (POLES,), jnp.float32, math.log(0.05), math.log(2.0))), 0.05, 2.0),
        "filter_weights": jnp.clip(jnp.exp(jax.random.uniform(splits[5], (POLES,), jnp.float32, math.log(0.03), math.log(0.3))), 0.03, 0.3),
    }


exact_mode = lax.Precision.HIGHEST


def apply_h(vector, hblocks, col_index):
    gathered = vector[col_index]
    forward = jnp.einsum("ikab,ikvb->iva", hblocks, gathered, precision=exact_mode)
    transposed = jnp.einsum("ikab,iva->ikvb", hblocks, vector, precision=exact_mode)
    backward = jax.ops.segment_sum(transposed.reshape(-1, vector.shape[1], vector.shape[2]), col_index.reshape(-1), num_segments=vector.shape[0])
    return forward + backward


def column_dot(first_arr, second_arr):
    return jnp.sum(first_arr * second_arr, axis=(0, 2))


def reference(hblocks, col_index, right_side, center, shifts, filter_weights):
    center_value = center[0]
    base_shift = jnp.min(shifts)
    delta_shift = (shifts - base_shift)[:, None]

    def operate(vector):
        shifted = apply_h(vector, hblocks, col_index) - center_value * vector
        return apply_h(shifted, hblocks, col_index) - center_value * shifted + base_shift * vector

    residual = right_side
    direction = right_side
    solutions = jnp.zeros((POLES,) + right_side.shape, jnp.float32)
    shifted_dirs = jnp.broadcast_to(right_side, solutions.shape)
    res_norm = column_dot(residual, residual)
    zeta_prev = jnp.ones((POLES, NVEC), jnp.float32)
    zeta_now = jnp.ones((POLES, NVEC), jnp.float32)
    alpha_prev = jnp.ones((NVEC,), jnp.float32)
    beta_prev = jnp.zeros((NVEC,), jnp.float32)
    for iteration in range(ITERS):
        op_image = operate(direction)
        alpha_now = res_norm / column_dot(direction, op_image)
        zeta_next = zeta_now * zeta_prev * alpha_prev / (alpha_now * beta_prev * (zeta_prev - zeta_now) + zeta_prev * alpha_prev * (1.0 + delta_shift * alpha_now))
        zeta_ratio = zeta_next / zeta_now
        solutions = solutions + (alpha_now * zeta_ratio)[:, None, :, None] * shifted_dirs
        residual = residual - alpha_now[None, :, None] * op_image
        if iteration + 1 < ITERS:
            norm_next = column_dot(residual, residual)
            beta_now = norm_next / res_norm
            direction = residual + beta_now[None, :, None] * direction
            shifted_dirs = zeta_next[:, None, :, None] * residual[None] + (beta_now * zeta_ratio * zeta_ratio)[:, None, :, None] * shifted_dirs
            zeta_prev, zeta_now, alpha_prev, beta_prev, res_norm = zeta_now, zeta_next, alpha_now, beta_now, norm_next
    filtered = jnp.sum(filter_weights[:, None, None, None] * solutions, axis=0)
    applied = apply_h(filtered, hblocks, col_index)
    row_total = NB * BLK
    gram_matrix = jnp.einsum("iae,ibe->ab", filtered, filtered, precision=exact_mode) / row_total
    ritz_matrix = jnp.einsum("iae,ibe->ab", filtered, applied, precision=exact_mode) / row_total
    return filtered, gram_matrix, ritz_matrix
```

```python
import jax
import jax.numpy as jnp
from jax import lax
from jax.sharding import PartitionSpec as P

CAP = 2


exact_mode = lax.Precision.HIGHEST


def column_dot(first_arr, second_arr):
    return jnp.sum(first_arr * second_arr, axis=(0, 2))


def ordered_lists(need_mask, slot_width):
    ranks = jnp.cumsum(need_mask, axis=1)
    positions = lax.broadcasted_iota(jnp.int32, need_mask.shape, 1)
    columns_out = []
    for slot in range(slot_width):
        hit = (need_mask > 0) & (ranks == slot + 1)
        columns_out.append(jnp.sum(jnp.where(hit, positions, 0), axis=1))
    lists = jnp.stack(columns_out, axis=1)
    live = jnp.sum(need_mask, axis=1, keepdims=True) > 0
    return jnp.where(live, lists, -1)


def filter_factors(alpha_one, beta_one, alpha_two, delta_shift, weights):
    zeta_one = 1.0 / (1.0 + delta_shift * alpha_one)
    zeta_two = (
        zeta_one
        * alpha_one
        / (alpha_two * beta_one * (1.0 - zeta_one) + alpha_one * (1.0 + delta_shift * alpha_two))
    )
    from_start = jnp.sum(
        weights * (alpha_one * zeta_one + alpha_two * beta_one * zeta_one * zeta_two), axis=0
    )
    from_residual = jnp.sum(weights * (alpha_two * zeta_two), axis=0)
    return from_start, from_residual


def shards(hblocks, col_index, right_side, center, shifts, filter_weights):
    block_rows = hblocks.shape[0]
    block_width = hblocks.shape[2]
    local_vecs = right_side.shape[1]
    pole_count = shifts.shape[0]
    peer_count = lax.axis_size("rows")
    slot_width = CAP
    device_index = lax.axis_index("rows")
    own_cols = col_index[:, :block_rows] - device_index * block_rows
    far_cols = col_index[:, block_rows:].reshape(-1)
    near_blocks = hblocks[:, :block_rows]
    far_blocks = hblocks[:, block_rows:]
    every_key = jnp.arange(peer_count * block_rows, dtype=jnp.int32)
    need_mask = (
        jnp.any(far_cols[:, None] == every_key[None, :], axis=0)
        .astype(jnp.int32)
        .reshape(peer_count, block_rows)
    )
    incoming_mask = lax.all_to_all(need_mask, "rows", split_axis=0, concat_axis=0, tiled=True)
    send_lists = ordered_lists(incoming_mask, slot_width)
    my_lists = ordered_lists(need_mask, slot_width)
    owners = lax.broadcasted_iota(jnp.int32, my_lists.shape, 0)
    slot_keys = jnp.where(my_lists >= 0, owners * block_rows + my_lists, -1).reshape(-1)
    slot_total = slot_keys.shape[0]
    matches = far_cols[:, None] == slot_keys[None, :]
    picker = matches.astype(jnp.float32)
    slot_numbers = lax.broadcasted_iota(jnp.int32, matches.shape, 1)
    slot_of_ref = jnp.sum(jnp.where(matches, slot_numbers, 0), axis=1)
    row_numbers = jnp.arange(block_rows, dtype=jnp.int32)[:, None]
    spread = (send_lists.reshape(-1)[None, :] == row_numbers).astype(jnp.float32)
    own_spread = (own_cols.reshape(-1)[None, :] == row_numbers).astype(jnp.float32)
    send_index = jnp.maximum(send_lists, 0)
    send_live = (send_lists >= 0)[:, :, None, None]

    def apply_h(vector):
        far_terms = jnp.einsum("ikab,iva->ikvb", far_blocks, vector, precision=exact_mode).reshape(
            far_cols.shape[0], -1
        )
        slot_sums = jnp.dot(picker.T, far_terms, precision=exact_mode).reshape(
            peer_count, slot_width, local_vecs, block_width
        )
        picked = vector[send_index]
        outgoing = jnp.where(send_live, picked, jnp.zeros_like(picked))
        both = lax.all_to_all(
            jnp.concatenate([outgoing, slot_sums], axis=1),
            "rows",
            split_axis=0,
            concat_axis=0,
            tiled=True,
        )
        arrived = both[:, :slot_width].reshape(slot_total, local_vecs, block_width)
        returned = both[:, slot_width:].reshape(slot_total, -1)
        near_vec = vector[own_cols]
        result = jnp.einsum("ikab,ikvb->iva", near_blocks, near_vec, precision=exact_mode)
        near_terms = jnp.einsum(
            "ikab,iva->ikvb", near_blocks, vector, precision=exact_mode
        ).reshape(block_rows * block_rows, -1)
        result = result + jnp.dot(own_spread, near_terms, precision=exact_mode).reshape(
            vector.shape
        )
        far_vec = arrived[slot_of_ref]
        far_vec = far_vec.reshape(block_rows, -1, local_vecs, block_width)
        result = result + jnp.einsum("ikab,ikvb->iva", far_blocks, far_vec, precision=exact_mode)
        return result + jnp.dot(spread, returned, precision=exact_mode).reshape(vector.shape)

    def wide(per_column):
        return per_column[None, :, None]

    center_value = center[0]
    base_shift = jnp.min(shifts)
    delta_shift = (shifts - base_shift)[:, None]
    start = right_side
    start_image = apply_h(start)
    half_one = start_image - center_value * start
    start_norm, half_norm = lax.psum(
        jnp.stack([column_dot(start, start), column_dot(half_one, half_one)]), "rows"
    )
    alpha_one = start_norm / (half_norm + base_shift * start_norm)
    op_image = apply_h(half_one) - center_value * half_one + base_shift * start
    residual = start - wide(alpha_one) * op_image
    residual_image = apply_h(residual)
    res_norm = lax.psum(column_dot(residual, residual), "rows")
    beta_one = res_norm / start_norm
    direction = residual + wide(beta_one) * start
    half_two = residual_image - center_value * residual + wide(beta_one) * half_one
    energy = lax.psum(
        column_dot(half_two, half_two) + base_shift * column_dot(direction, direction), "rows"
    )
    from_start, from_residual = filter_factors(
        alpha_one, beta_one, res_norm / energy, delta_shift, filter_weights[:, None]
    )
    filtered = wide(from_start) * start + wide(from_residual) * residual
    applied = wide(from_start) * start_image + wide(from_residual) * residual_image
    column_piece = lax.all_gather(filtered, "cols", axis=1, tiled=True)
    correlation = jnp.einsum("iae,ibe->ab", column_piece, filtered, precision=exact_mode)
    projected = jnp.einsum("iae,ibe->ab", column_piece, applied, precision=exact_mode)
    partial_gram = jnp.stack([correlation, projected])
    summed = lax.psum(partial_gram, "rows")
    row_total = peer_count * block_rows * block_width
    return (filtered, summed[0] / row_total, summed[1] / row_total)


def solution(mesh):
    placed = (P("rows", None, None, None), P("rows", None), P("rows", "cols", None), P(), P(), P())
    return jax.shard_map(
        shards,
        mesh=mesh,
        in_specs=placed,
        out_specs=(P("rows", "cols", None), P(None, "cols"), P(None, "cols")),
        check_vma=False,
    )
```

```python
import functools

import jax
import jax.numpy as jnp
from jax import lax
from jax.experimental import pallas as pl
from jax.experimental.pallas import tpu as pltpu
from jax.sharding import PartitionSpec as P

CAP = 2


exact_mode = lax.Precision.HIGHEST


def column_dot(first_arr, second_arr):
    return jnp.sum(first_arr * second_arr, axis=(0, 2))


def ordered_lists(need_mask, slot_width):
    ranks = jnp.cumsum(need_mask, axis=1)
    positions = lax.broadcasted_iota(jnp.int32, need_mask.shape, 1)
    columns_out = []
    for slot in range(slot_width):
        hit = (need_mask > 0) & (ranks == slot + 1)
        columns_out.append(jnp.sum(jnp.where(hit, positions, 0), axis=1))
    lists = jnp.stack(columns_out, axis=1)
    live = jnp.sum(need_mask, axis=1, keepdims=True) > 0
    return jnp.where(live, lists, -1)


def filter_factors(alpha_one, beta_one, alpha_two, delta_shift, weights):
    zeta_one = 1.0 / (1.0 + delta_shift * alpha_one)
    zeta_two = (
        zeta_one
        * alpha_one
        / (alpha_two * beta_one * (1.0 - zeta_one) + alpha_one * (1.0 + delta_shift * alpha_two))
    )
    from_start = jnp.sum(
        weights * (alpha_one * zeta_one + alpha_two * beta_one * zeta_one * zeta_two), axis=0
    )
    from_residual = jnp.sum(weights * (alpha_two * zeta_two), axis=0)
    return from_start, from_residual


def shards(hblocks, col_index, right_side, center, shifts, filter_weights):
    block_rows = hblocks.shape[0]
    block_width = hblocks.shape[2]
    local_vecs = right_side.shape[1]
    pole_count = shifts.shape[0]
    peer_count = lax.axis_size("rows")
    slot_width = CAP
    device_index = lax.axis_index("rows")
    own_cols = col_index[:, :block_rows] - device_index * block_rows
    far_cols = col_index[:, block_rows:].reshape(-1)
    near_blocks = hblocks[:, :block_rows]
    far_blocks = hblocks[:, block_rows:]
    every_key = jnp.arange(peer_count * block_rows, dtype=jnp.int32)
    need_mask = (
        jnp.any(far_cols[:, None] == every_key[None, :], axis=0)
        .astype(jnp.int32)
        .reshape(peer_count, block_rows)
    )
    incoming_mask = lax.all_to_all(need_mask, "rows", split_axis=0, concat_axis=0, tiled=True)
    send_lists = ordered_lists(incoming_mask, slot_width)
    my_lists = ordered_lists(need_mask, slot_width)
    owners = lax.broadcasted_iota(jnp.int32, my_lists.shape, 0)
    slot_keys = jnp.where(my_lists >= 0, owners * block_rows + my_lists, -1).reshape(-1)
    slot_total = slot_keys.shape[0]
    matches = far_cols[:, None] == slot_keys[None, :]
    picker = matches.astype(jnp.float32)
    slot_numbers = lax.broadcasted_iota(jnp.int32, matches.shape, 1)
    slot_of_ref = jnp.sum(jnp.where(matches, slot_numbers, 0), axis=1)
    row_numbers = jnp.arange(block_rows, dtype=jnp.int32)[:, None]
    spread = (send_lists.reshape(-1)[None, :] == row_numbers).astype(jnp.float32)
    own_spread = (own_cols.reshape(-1)[None, :] == row_numbers).astype(jnp.float32)
    send_index = jnp.maximum(send_lists, 0)
    send_live = (send_lists >= 0)[:, :, None, None]

    def apply_h(vector):
        far_terms = jnp.einsum("ikab,iva->ikvb", far_blocks, vector, precision=exact_mode).reshape(
            far_cols.shape[0], -1
        )
        slot_sums = jnp.dot(picker.T, far_terms, precision=exact_mode).reshape(
            peer_count, slot_width, local_vecs, block_width
        )
        picked = vector[send_index]
        outgoing = jnp.where(send_live, picked, jnp.zeros_like(picked))
        both = lax.all_to_all(
            jnp.concatenate([outgoing, slot_sums], axis=1),
            "rows",
            split_axis=0,
            concat_axis=0,
            tiled=True,
        )
        arrived = both[:, :slot_width].reshape(slot_total, local_vecs, block_width)
        returned = both[:, slot_width:].reshape(slot_total, -1)
        near_vec = vector[own_cols]
        result = jnp.einsum("ikab,ikvb->iva", near_blocks, near_vec, precision=exact_mode)
        near_terms = jnp.einsum(
            "ikab,iva->ikvb", near_blocks, vector, precision=exact_mode
        ).reshape(block_rows * block_rows, -1)
        result = result + jnp.dot(own_spread, near_terms, precision=exact_mode).reshape(
            vector.shape
        )
        far_vec = arrived[slot_of_ref]
        far_vec = far_vec.reshape(block_rows, -1, local_vecs, block_width)
        result = result + jnp.einsum("ikab,ikvb->iva", far_blocks, far_vec, precision=exact_mode)
        return result + jnp.dot(spread, returned, precision=exact_mode).reshape(vector.shape)

    def wide(per_column):
        return per_column[None, :, None]

    center_value = center[0]
    base_shift = jnp.min(shifts)
    delta_shift = (shifts - base_shift)[:, None]
    start = right_side
    start_image = apply_h(start)
    half_one = start_image - center_value * start
    start_norm, half_norm = lax.psum(
        jnp.stack([column_dot(start, start), column_dot(half_one, half_one)]), "rows"
    )
    alpha_one = start_norm / (half_norm + base_shift * start_norm)
    op_image = apply_h(half_one) - center_value * half_one + base_shift * start
    residual = start - wide(alpha_one) * op_image
    residual_image = apply_h(residual)
    res_norm = lax.psum(column_dot(residual, residual), "rows")
    beta_one = res_norm / start_norm
    direction = residual + wide(beta_one) * start
    half_two = residual_image - center_value * residual + wide(beta_one) * half_one
    energy = lax.psum(
        column_dot(half_two, half_two) + base_shift * column_dot(direction, direction), "rows"
    )
    from_start, from_residual = filter_factors(
        alpha_one, beta_one, res_norm / energy, delta_shift, filter_weights[:, None]
    )
    filtered = wide(from_start) * start + wide(from_residual) * residual
    applied = wide(from_start) * start_image + wide(from_residual) * residual_image
    column_piece = lax.all_gather(filtered, "cols", axis=1, tiled=True)
    correlation = jnp.einsum("iae,ibe->ab", column_piece, filtered, precision=exact_mode)
    projected = jnp.einsum("iae,ibe->ab", column_piece, applied, precision=exact_mode)
    partial_gram = jnp.stack([correlation, projected])
    summed = lax.psum(partial_gram, "rows")
    row_total = peer_count * block_rows * block_width
    return (filtered, summed[0] / row_total, summed[1] / row_total)


def split(value):
    high = value.astype(jnp.bfloat16)
    low = (value - high.astype(jnp.float32)).astype(jnp.bfloat16)
    return high, low


def pack_kernel(index_ref, blocks_ref, high_ref, low_ref, acc):
    row = pl.program_id(0)
    width = blocks_ref.shape[-1]
    acc[...] = jnp.zeros_like(acc)
    for k in range(blocks_ref.shape[1]):
        spot = index_ref[row, k]
        acc[spot] = acc[spot] + blocks_ref[0, k]
    for spot in range(acc.shape[0]):
        high, low = split(acc[spot])
        high_ref[:, spot * width : (spot + 1) * width] = high
        low_ref[:, spot * width : (spot + 1) * width] = low


def pack_blocks(index, hblocks, spots):
    block_rows, per_row, width, _ = hblocks.shape
    out = jax.ShapeDtypeStruct((block_rows * width, spots * width), jnp.bfloat16)
    out_spec = pl.BlockSpec((width, spots * width), lambda i, index_ref: (i, 0))
    return pl.pallas_call(
        pack_kernel,
        grid_spec=pltpu.PrefetchScalarGridSpec(
            num_scalar_prefetch=1,
            grid=(block_rows,),
            in_specs=[
                pl.BlockSpec((1, per_row, width, width), lambda i, index_ref: (i, 0, 0, 0))
            ],
            out_specs=[out_spec, out_spec],
            scratch_shapes=[pltpu.VMEM((spots, width, width), jnp.float32)],
        ),
        out_shape=[out, out],
        compiler_params=pltpu.CompilerParams(vmem_limit_bytes=16 << 20),
    )(index, hblocks)


def filter_kernel(
    n_rows,
    n_cols,
    center_ref,
    shifts_ref,
    weights_ref,
    vec_ref,
    lists_ref,
    high_hbm,
    low_hbm,
    out_ref,
    gram_ref,
    ritz_ref,
    high,
    low,
    lists,
    first_send,
    first_recv,
    vec_send,
    vec_recv,
    prod_send,
    prod_recv,
    col_start,
    col_res,
    res_send,
    energy_send,
    energy_recv,
    factor_send,
    factors,
    gram_send,
    gram_recv,
    load_sem,
    list_sems,
    vec_sems,
    prod_sems,
    col_sems,
    energy_sems,
    gram_sems,
):
    block_rows, vecs, width = vec_ref.shape
    mine = block_rows * width
    pair = CAP * width
    peers = n_rows - 1
    me = lax.axis_index("rows")
    me_col = lax.axis_index("cols")
    pending = []

    loads = [
        pltpu.make_async_copy(high_hbm, high, load_sem.at[0]),
        pltpu.make_async_copy(low_hbm, low, load_sem.at[1]),
    ]
    for load in loads:
        load.start()

    barrier = pltpu.get_barrier_semaphore()
    for step in range(1, n_rows):
        pl.semaphore_signal(barrier, inc=1, device_id={"rows": lax.rem(me + step, n_rows)})
    for step in range(1, n_cols):
        pl.semaphore_signal(barrier, inc=1, device_id={"cols": lax.rem(me_col + step, n_cols)})
    pl.semaphore_wait(barrier, peers + n_cols - 1)

    def to_row(src, dst, sems, step):
        copy = pltpu.make_async_remote_copy(
            src_ref=src,
            dst_ref=dst,
            send_sem=sems.at[0, step - 1],
            recv_sem=sems.at[1, peers - step],
            device_id={"rows": lax.rem(me + step, n_rows)},
            device_id_type=pl.DeviceIdType.MESH,
        )
        copy.start()
        pending.append(copy)
        return copy

    def to_col(src, dst, sems, step):
        copy = pltpu.make_async_remote_copy(
            src_ref=src,
            dst_ref=dst,
            send_sem=sems.at[0, step - 1],
            recv_sem=sems.at[1, n_cols - 1 - step],
            device_id={"cols": lax.rem(me_col + step, n_cols)},
            device_id_type=pl.DeviceIdType.MESH,
        )
        copy.start()
        pending.append(copy)
        return copy

    def arrive(copies):
        for copy in copies:
            copy.wait_recv()

    list_copies = [
        to_row(lists_ref.at[step - 1], lists.at[peers - step], list_sems, step)
        for step in range(1, n_rows)
    ]

    def flat(ref):
        return jnp.concatenate([ref[i] for i in range(block_rows)], axis=1)

    start = flat(vec_ref)

    def named(step, slot, row):
        mask = lists[step - 1, slot] == row
        return jnp.concatenate([mask.astype(jnp.float32)] * (vecs // 8), axis=0) > 0.5

    def dot(a, b, transposed):
        return lax.dot_general(
            a, b, (((1,), (1 if transposed else 0,)), ((), ())),
            preferred_element_type=jnp.float32,
        )

    def times(both, top, columns, transposed):
        wide_part = dot(both, high[:, columns], transposed)
        count = top.shape[0]
        return wide_part[:count] + wide_part[count:] + dot(top, low[:, columns], transposed)

    def apply_h(turn, vector, extra):
        copies = []
        for step in range(1, n_rows):
            parts = []
            for slot in range(CAP):
                picked = jnp.zeros((vecs, width), jnp.float32)
                for row in range(block_rows):
                    piece = vector[:, row * width : (row + 1) * width]
                    picked = jnp.where(named(step, slot, row), piece, picked)
                parts.append(picked)
            if extra is None:
                out, into = first_send.at[step - 1], first_recv.at[peers - step]
            else:
                parts.append(extra)
                out, into = vec_send.at[turn - 1, step - 1], vec_recv.at[turn - 1, peers - step]
            out[...] = jnp.concatenate(parts, axis=1)
            copies.append(to_row(out, into, vec_sems.at[turn], step))
        top, bottom = split(vector)
        both = jnp.concatenate([top, bottom], axis=0)
        if turn == 0:
            for load in loads:
                load.wait()
        products = []
        for step in range(1, n_rows):
            columns = slice(mine + (step - 1) * pair, mine + step * pair)
            prod_send[turn, step - 1] = times(both, top, columns, False)
            products.append(
                to_row(
                    prod_send.at[turn, step - 1],
                    prod_recv.at[turn, peers - step],
                    prod_sems.at[turn],
                    step,
                )
            )
        near = slice(0, mine)
        result = times(both, top, near, False) + times(both, top, near, True)
        arrive(copies)
        source = first_recv if extra is None else vec_recv.at[turn - 1]
        far = jnp.concatenate([source[step - 1, :, :pair] for step in range(1, n_rows)], axis=1)
        total = extra
        if extra is not None:
            for step in range(1, n_rows):
                total = total + source[step - 1, :, pair:]
        top, bottom = split(far)
        both = jnp.concatenate([top, bottom], axis=0)
        result = result + times(both, top, slice(mine, mine + peers * pair), True)
        arrive(products)
        pieces = []
        for row in range(block_rows):
            piece = result[:, row * width : (row + 1) * width]
            for step in range(1, n_rows):
                for slot in range(CAP):
                    back = prod_recv[turn, step - 1, :, slot * width : (slot + 1) * width]
                    piece = piece + jnp.where(named(step, slot, row), back, 0.0)
            pieces.append(piece)
        return jnp.concatenate(pieces, axis=1), total

    def column_sum(value):
        return jnp.sum(value, axis=1, keepdims=True)

    center = center_ref[0]
    poles = [shifts_ref[m] for m in range(shifts_ref.shape[0])]
    base = functools.reduce(jnp.minimum, poles)
    lane = lax.broadcasted_iota(jnp.int32, (vecs, width), 1)
    all_lanes = jnp.zeros((vecs, width), jnp.float32)

    col_copies = [
        to_col(vec_ref, col_start.at[me_col], col_sems.at[0], step) for step in range(1, n_cols)
    ]
    col_start[me_col] = vec_ref[...]
    arrive(list_copies)
    start_image, _ = apply_h(0, start, None)
    half_one = start_image - center * start
    own_sums = jnp.where(lane == 0, column_sum(start * start), column_sum(half_one * half_one))
    second, sums = apply_h(1, half_one, own_sums)
    start_norm = sums[:, 0:1]
    half_norm = sums[:, 1:2]
    alpha_one = start_norm / (half_norm + base * start_norm)
    op_image = second - center * half_one + base * start
    residual = start - alpha_one * op_image
    for row in range(block_rows):
        res_send[row] = residual[:, row * width : (row + 1) * width]
    col_res[me_col] = res_send[...]
    col_copies += [
        to_col(res_send, col_res.at[me_col], col_sems.at[1], step) for step in range(1, n_cols)
    ]
    own_norm = column_sum(residual * residual) + all_lanes
    residual_image, sums = apply_h(2, residual, own_norm)
    res_norm = sums[:, 0:1]
    beta = res_norm / start_norm
    direction = residual + beta * start
    half_two = residual_image - center * residual + beta * half_one
    own_energy = column_sum(half_two * half_two + base * (direction * direction)) + all_lanes
    energy_send[...] = own_energy
    energy_copies = [
        to_row(energy_send, energy_recv.at[peers - step], energy_sems, step)
        for step in range(1, n_rows)
    ]
    arrive(energy_copies)
    energy = own_energy
    for step in range(1, n_rows):
        energy = energy + energy_recv[step - 1]
    alpha_one = alpha_one + all_lanes
    beta = beta + all_lanes
    alpha_two = res_norm / energy
    from_start = all_lanes
    from_residual = all_lanes
    for m, pole in enumerate(poles):
        delta = pole - base
        zeta_one = 1.0 / (1.0 + delta * alpha_one)
        zeta_two = (
            zeta_one
            * alpha_one
            / (
                alpha_two * beta * (1.0 - zeta_one)
                + alpha_one * (1.0 + delta * alpha_two)
            )
        )
        weight = weights_ref[m]
        from_start = from_start + weight * (
            alpha_one * zeta_one + alpha_two * beta * zeta_one * zeta_two
        )
        from_residual = from_residual + weight * (alpha_two * zeta_two)
    factor_send[...] = jnp.where(lane == 0, from_start, from_residual)
    factors[me_col] = factor_send[...]
    col_copies += [
        to_col(factor_send, factors.at[me_col], col_sems.at[2], step)
        for step in range(1, n_cols)
    ]
    along_start, along_res = from_start[:, 0:1], from_residual[:, 0:1]
    filtered = along_start * start + along_res * residual
    applied = along_start * start_image + along_res * residual_image
    for row in range(block_rows):
        out_ref[row] = filtered[:, row * width : (row + 1) * width]
    own = jnp.concatenate([filtered, applied], axis=0)
    arrive(col_copies)
    every = jnp.concatenate(
        [
            factors[c, :, 0:1] * flat(col_start.at[c]) + factors[c, :, 1:2] * flat(col_res.at[c])
            for c in range(n_cols)
        ],
        axis=0,
    )
    top, bottom = split(own)
    every_top, every_bottom = split(every)
    both = dot(jnp.concatenate([top, bottom], axis=0), every_top, True)
    count = 2 * vecs
    partial = both[:count] + both[count:] + dot(top, every_bottom, True)
    gram_send[...] = jnp.concatenate([partial[:vecs], partial[vecs:]], axis=1)
    gram_recv[me] = gram_send[...]
    gram_copies = [
        to_row(gram_send, gram_recv.at[me], gram_sems, step) for step in range(1, n_rows)
    ]
    arrive(gram_copies)
    summed = gram_recv[0]
    for device in range(1, n_rows):
        summed = summed + gram_recv[device]
    turned = jnp.transpose(summed * (1.0 / (n_rows * mine)))
    columns = n_cols * vecs
    gram_ref[...] = turned[:columns]
    ritz_ref[...] = turned[columns:]
    for copy in pending:
        copy.wait_send()


def fused_shards(
    n_rows, n_cols, hblocks, col_index, right_side, center, shifts, filter_weights
):
    block_rows, _, width, _ = hblocks.shape
    vecs = right_side.shape[1]
    peers = n_rows - 1
    spots = block_rows + CAP * peers
    mine = block_rows * width
    me = lax.axis_index("rows")
    far = col_index[:, block_rows:]
    owner = far // block_rows
    row = far - owner * block_rows
    ahead = lax.rem(owner - me + n_rows, n_rows)
    hit = ahead[None] == jnp.arange(1, n_rows, dtype=jnp.int32)[:, None, None]
    low_row = jnp.min(jnp.where(hit, row[None], block_rows), axis=(1, 2))
    high_row = jnp.max(jnp.where(hit, row[None], -1), axis=(1, 2))
    last = jnp.sum(jnp.where(hit, high_row[:, None, None], 0), axis=0)
    slot = block_rows + CAP * (ahead - 1) + (row == last).astype(jnp.int32)
    index = jnp.concatenate([col_index[:, :block_rows] - me * block_rows, slot], axis=1)
    lists = jnp.broadcast_to(
        jnp.stack([low_row, high_row], axis=1)[:, :, None, None], (peers, CAP, 8, width)
    )
    high, low = pack_blocks(index, hblocks, spots)
    columns = n_cols * vecs
    pair = CAP * width
    vmem = pl.BlockSpec(memory_space=pltpu.VMEM)
    smem = pl.BlockSpec(memory_space=pltpu.SMEM)
    anywhere = pl.BlockSpec(memory_space=pl.ANY)
    f32 = jnp.float32
    return pl.pallas_call(
        functools.partial(filter_kernel, n_rows, n_cols),
        out_shape=[
            jax.ShapeDtypeStruct(right_side.shape, f32),
            jax.ShapeDtypeStruct((columns, vecs), f32),
            jax.ShapeDtypeStruct((columns, vecs), f32),
        ],
        in_specs=[smem, smem, smem, vmem, vmem, anywhere, anywhere],
        out_specs=[vmem, vmem, vmem],
        scratch_shapes=[
            pltpu.VMEM((mine, spots * width), jnp.bfloat16),
            pltpu.VMEM((mine, spots * width), jnp.bfloat16),
            pltpu.VMEM((peers, CAP, 8, width), jnp.int32),
            pltpu.VMEM((peers, vecs, pair), f32),
            pltpu.VMEM((peers, vecs, pair), f32),
            pltpu.VMEM((2, peers, vecs, pair + width), f32),
            pltpu.VMEM((2, peers, vecs, pair + width), f32),
            pltpu.VMEM((3, peers, vecs, pair), f32),
            pltpu.VMEM((3, peers, vecs, pair), f32),
            pltpu.VMEM((n_cols,) + right_side.shape, f32),
            pltpu.VMEM((n_cols,) + right_side.shape, f32),
            pltpu.VMEM(right_side.shape, f32),
            pltpu.VMEM((vecs, width), f32),
            pltpu.VMEM((peers, vecs, width), f32),
            pltpu.VMEM((vecs, width), f32),
            pltpu.VMEM((n_cols, vecs, width), f32),
            pltpu.VMEM((vecs, 2 * columns), f32),
            pltpu.VMEM((n_rows, vecs, 2 * columns), f32),
            pltpu.SemaphoreType.DMA((2,)),
            pltpu.SemaphoreType.DMA((2, peers)),
            pltpu.SemaphoreType.DMA((3, 2, peers)),
            pltpu.SemaphoreType.DMA((3, 2, peers)),
            pltpu.SemaphoreType.DMA((3, 2, n_cols - 1)),
            pltpu.SemaphoreType.DMA((2, peers)),
            pltpu.SemaphoreType.DMA((2, peers)),
        ],
        compiler_params=pltpu.CompilerParams(
            collective_id=0, has_side_effects=True, vmem_limit_bytes=40 << 20
        ),
    )(center, shifts, filter_weights, right_side, lists, high, low)


def solution(mesh):
    placed = (P("rows", None, None, None), P("rows", None), P("rows", "cols", None), P(), P(), P())
    n_rows, n_cols = mesh.shape["rows"], mesh.shape["cols"]

    def body(hblocks, *rest):
        block_rows, per_row = hblocks.shape[:2]
        if CAP * (n_rows - 1) * block_rows <= block_rows * per_row:
            return fused_shards(n_rows, n_cols, hblocks, *rest)
        return shards(hblocks, *rest)

    return jax.shard_map(
        body,
        mesh=mesh,
        in_specs=placed,
        out_specs=(P("rows", "cols", None), P(None, "cols"), P(None, "cols")),
        check_vma=False,
    )
```

```python
import functools

import jax
import jax.numpy as jnp
from jax import lax
from jax.experimental import pallas as pl
from jax.experimental.pallas import tpu as pltpu
from jax.sharding import PartitionSpec as P

CAP = 2


exact_mode = lax.Precision.HIGHEST


def column_dot(first_arr, second_arr):
    return jnp.sum(first_arr * second_arr, axis=(0, 2))


def ordered_lists(need_mask, slot_width):
    ranks = jnp.cumsum(need_mask, axis=1)
    positions = lax.broadcasted_iota(jnp.int32, need_mask.shape, 1)
    columns_out = []
    for slot in range(slot_width):
        hit = (need_mask > 0) & (ranks == slot + 1)
        columns_out.append(jnp.sum(jnp.where(hit, positions, 0), axis=1))
    lists = jnp.stack(columns_out, axis=1)
    live = jnp.sum(need_mask, axis=1, keepdims=True) > 0
    return jnp.where(live, lists, -1)


def filter_factors(alpha_one, beta_one, alpha_two, delta_shift, weights):
    zeta_one = 1.0 / (1.0 + delta_shift * alpha_one)
    zeta_two = (
        zeta_one
        * alpha_one
        / (alpha_two * beta_one * (1.0 - zeta_one) + alpha_one * (1.0 + delta_shift * alpha_two))
    )
    from_start = jnp.sum(
        weights * (alpha_one * zeta_one + alpha_two * beta_one * zeta_one * zeta_two), axis=0
    )
    from_residual = jnp.sum(weights * (alpha_two * zeta_two), axis=0)
    return from_start, from_residual


def shards(hblocks, col_index, right_side, center, shifts, filter_weights):
    block_rows = hblocks.shape[0]
    block_width = hblocks.shape[2]
    local_vecs = right_side.shape[1]
    pole_count = shifts.shape[0]
    peer_count = lax.axis_size("rows")
    slot_width = CAP
    device_index = lax.axis_index("rows")
    own_cols = col_index[:, :block_rows] - device_index * block_rows
    far_cols = col_index[:, block_rows:].reshape(-1)
    near_blocks = hblocks[:, :block_rows]
    far_blocks = hblocks[:, block_rows:]
    every_key = jnp.arange(peer_count * block_rows, dtype=jnp.int32)
    need_mask = (
        jnp.any(far_cols[:, None] == every_key[None, :], axis=0)
        .astype(jnp.int32)
        .reshape(peer_count, block_rows)
    )
    incoming_mask = lax.all_to_all(need_mask, "rows", split_axis=0, concat_axis=0, tiled=True)
    send_lists = ordered_lists(incoming_mask, slot_width)
    my_lists = ordered_lists(need_mask, slot_width)
    owners = lax.broadcasted_iota(jnp.int32, my_lists.shape, 0)
    slot_keys = jnp.where(my_lists >= 0, owners * block_rows + my_lists, -1).reshape(-1)
    slot_total = slot_keys.shape[0]
    matches = far_cols[:, None] == slot_keys[None, :]
    picker = matches.astype(jnp.float32)
    slot_numbers = lax.broadcasted_iota(jnp.int32, matches.shape, 1)
    slot_of_ref = jnp.sum(jnp.where(matches, slot_numbers, 0), axis=1)
    row_numbers = jnp.arange(block_rows, dtype=jnp.int32)[:, None]
    spread = (send_lists.reshape(-1)[None, :] == row_numbers).astype(jnp.float32)
    own_spread = (own_cols.reshape(-1)[None, :] == row_numbers).astype(jnp.float32)
    send_index = jnp.maximum(send_lists, 0)
    send_live = (send_lists >= 0)[:, :, None, None]

    def apply_h(vector):
        far_terms = jnp.einsum("ikab,iva->ikvb", far_blocks, vector, precision=exact_mode).reshape(
            far_cols.shape[0], -1
        )
        slot_sums = jnp.dot(picker.T, far_terms, precision=exact_mode).reshape(
            peer_count, slot_width, local_vecs, block_width
        )
        picked = vector[send_index]
        outgoing = jnp.where(send_live, picked, jnp.zeros_like(picked))
        both = lax.all_to_all(
            jnp.concatenate([outgoing, slot_sums], axis=1),
            "rows",
            split_axis=0,
            concat_axis=0,
            tiled=True,
        )
        arrived = both[:, :slot_width].reshape(slot_total, local_vecs, block_width)
        returned = both[:, slot_width:].reshape(slot_total, -1)
        near_vec = vector[own_cols]
        result = jnp.einsum("ikab,ikvb->iva", near_blocks, near_vec, precision=exact_mode)
        near_terms = jnp.einsum(
            "ikab,iva->ikvb", near_blocks, vector, precision=exact_mode
        ).reshape(block_rows * block_rows, -1)
        result = result + jnp.dot(own_spread, near_terms, precision=exact_mode).reshape(
            vector.shape
        )
        far_vec = arrived[slot_of_ref]
        far_vec = far_vec.reshape(block_rows, -1, local_vecs, block_width)
        result = result + jnp.einsum("ikab,ikvb->iva", far_blocks, far_vec, precision=exact_mode)
        return result + jnp.dot(spread, returned, precision=exact_mode).reshape(vector.shape)

    def wide(per_column):
        return per_column[None, :, None]

    center_value = center[0]
    base_shift = jnp.min(shifts)
    delta_shift = (shifts - base_shift)[:, None]
    start = right_side
    start_image = apply_h(start)
    half_one = start_image - center_value * start
    start_norm, half_norm = lax.psum(
        jnp.stack([column_dot(start, start), column_dot(half_one, half_one)]), "rows"
    )
    alpha_one = start_norm / (half_norm + base_shift * start_norm)
    op_image = apply_h(half_one) - center_value * half_one + base_shift * start
    residual = start - wide(alpha_one) * op_image
    residual_image = apply_h(residual)
    res_norm = lax.psum(column_dot(residual, residual), "rows")
    beta_one = res_norm / start_norm
    direction = residual + wide(beta_one) * start
    half_two = residual_image - center_value * residual + wide(beta_one) * half_one
    energy = lax.psum(
        column_dot(half_two, half_two) + base_shift * column_dot(direction, direction), "rows"
    )
    from_start, from_residual = filter_factors(
        alpha_one, beta_one, res_norm / energy, delta_shift, filter_weights[:, None]
    )
    filtered = wide(from_start) * start + wide(from_residual) * residual
    applied = wide(from_start) * start_image + wide(from_residual) * residual_image
    column_piece = lax.all_gather(filtered, "cols", axis=1, tiled=True)
    correlation = jnp.einsum("iae,ibe->ab", column_piece, filtered, precision=exact_mode)
    projected = jnp.einsum("iae,ibe->ab", column_piece, applied, precision=exact_mode)
    partial_gram = jnp.stack([correlation, projected])
    summed = lax.psum(partial_gram, "rows")
    row_total = peer_count * block_rows * block_width
    return (filtered, summed[0] / row_total, summed[1] / row_total)


def split(value):
    high = value.astype(jnp.bfloat16)
    low = (value - high.astype(jnp.float32)).astype(jnp.bfloat16)
    return high, low


def pack_kernel(
    n_rows,
    me_ref,
    cols_ref,
    blocks_hbm,
    high_ref,
    low_ref,
    lists_ref,
    blocks,
    acc,
    index,
    scalars,
    sem,
    load_sems,
):
    width = blocks.shape[-1]
    block_rows, per_row = cols_ref.shape
    me = me_ref[0]

    def load(row):
        return pltpu.make_async_copy(blocks_hbm.at[row], blocks.at[row], load_sems.at[row])

    for row in range(block_rows):
        load(row).start()

    def place_blocks():
        columns = cols_ref[...].astype(jnp.float32)
        place = lax.broadcasted_iota(jnp.int32, columns.shape, 1)
        spots = columns - (me * block_rows).astype(jnp.float32)
        for step in range(1, n_rows):
            first = (lax.rem(me + step, n_rows) * block_rows).astype(jnp.float32)
            inner = columns - first
            hit = (place >= block_rows) & (inner >= 0.0) & (inner < block_rows)
            low_row = jnp.where(hit, inner, float(block_rows))
            low_row = jnp.min(jnp.min(low_row, axis=1, keepdims=True), axis=0, keepdims=True)
            high_row = jnp.where(hit, inner, -1.0)
            high_row = jnp.max(jnp.max(high_row, axis=1, keepdims=True), axis=0, keepdims=True)
            slot = float(block_rows + CAP * (step - 1)) + jnp.where(inner == high_row, 1.0, 0.0)
            spots = jnp.where(hit, slot, spots)
            lists_ref[step - 1, 0:1, :] = jnp.broadcast_to(low_row, (1, width))
            lists_ref[step - 1, 1:2, :] = jnp.broadcast_to(high_row, (1, width))
        index[...] = jnp.zeros_like(index)
        index[:, :per_row] = spots.astype(jnp.int32)
        move = pltpu.make_async_copy(index, scalars, sem)
        move.start()
        move.wait()

    place_blocks()

    @pl.loop(0, block_rows)
    def _(row):
        acc[...] = jnp.zeros_like(acc)
        load(row).wait()
        for k in range(per_row):
            spot = scalars[row, k]
            acc[spot] = acc[spot] + blocks[row, k]
        lines = pl.ds(pl.multiple_of(row * width, width), width)
        for spot in range(acc.shape[0]):
            high, low = split(acc[spot])
            high_ref[lines, spot * width : (spot + 1) * width] = high
            low_ref[lines, spot * width : (spot + 1) * width] = low


def pack_blocks(n_rows, me, col_index, hblocks, spots):
    block_rows, per_row, width, _ = hblocks.shape
    out = jax.ShapeDtypeStruct((block_rows * width, spots * width), jnp.bfloat16)
    lists = (n_rows - 1, CAP, width)
    vmem = pl.BlockSpec(memory_space=pltpu.VMEM)
    return pl.pallas_call(
        functools.partial(pack_kernel, n_rows),
        in_specs=[
            pl.BlockSpec(memory_space=pltpu.SMEM),
            vmem,
            pl.BlockSpec(memory_space=pltpu.HBM),
        ],
        out_specs=[vmem, vmem, vmem],
        scratch_shapes=[
            pltpu.VMEM(hblocks.shape, jnp.float32),
            pltpu.VMEM((spots, width, width), jnp.float32),
            pltpu.VMEM((block_rows, 128), jnp.int32),
            pltpu.SMEM((block_rows, 128), jnp.int32),
            pltpu.SemaphoreType.DMA,
            pltpu.SemaphoreType.DMA((block_rows,)),
        ],
        out_shape=[out, out, jax.ShapeDtypeStruct(lists, jnp.float32)],
        compiler_params=pltpu.CompilerParams(vmem_limit_bytes=36 << 20),
    )(me, col_index, hblocks)


def filter_kernel(
    n_rows,
    n_cols,
    center_ref,
    shifts_ref,
    weights_ref,
    vec_ref,
    lists_ref,
    high,
    low,
    out_ref,
    gram_ref,
    ritz_ref,
    lists,
    vec_send,
    vec_recv,
    prod_send,
    prod_recv,
    col_start,
    col_res,
    res_send,
    sums_send,
    sums_recv,
    factor_send,
    factors,
    gram_send,
    gram_recv,
    list_sems,
    vec_sems,
    prod_sems,
    col_sems,
    sums_sems,
    gram_sems,
):
    block_rows, vecs, width = vec_ref.shape
    mine = block_rows * width
    pair = CAP * width
    peers = n_rows - 1
    me = lax.axis_index("rows")
    me_col = lax.axis_index("cols")
    pending = []

    barrier = pltpu.get_barrier_semaphore()
    for step in range(1, n_rows):
        pl.semaphore_signal(barrier, inc=1, device_id={"rows": lax.rem(me + step, n_rows)})
    for step in range(1, n_cols):
        pl.semaphore_signal(barrier, inc=1, device_id={"cols": lax.rem(me_col + step, n_cols)})
    pl.semaphore_wait(barrier, peers + n_cols - 1)

    def to_row(src, dst, sems, step):
        copy = pltpu.make_async_remote_copy(
            src_ref=src,
            dst_ref=dst,
            send_sem=sems.at[0, step - 1],
            recv_sem=sems.at[1, peers - step],
            device_id={"rows": lax.rem(me + step, n_rows)},
            device_id_type=pl.DeviceIdType.MESH,
        )
        copy.start()
        pending.append(copy)
        return copy

    def to_col(src, dst, sems, step):
        copy = pltpu.make_async_remote_copy(
            src_ref=src,
            dst_ref=dst,
            send_sem=sems.at[0, step - 1],
            recv_sem=sems.at[1, n_cols - 1 - step],
            device_id={"cols": lax.rem(me_col + step, n_cols)},
            device_id_type=pl.DeviceIdType.MESH,
        )
        copy.start()
        pending.append(copy)
        return copy

    def arrive(copies):
        for copy in copies:
            copy.wait_recv()

    list_copies = [
        to_row(lists_ref.at[step - 1], lists.at[peers - step], list_sems, step)
        for step in range(1, n_rows)
    ]

    def flat(ref):
        return jnp.concatenate([ref[i] for i in range(block_rows)], axis=1)

    start = flat(vec_ref)

    def named(step, slot, row):
        return jnp.broadcast_to(lists[step - 1, slot : slot + 1, :], (vecs, width)) == float(row)

    def dot(a, b, transposed):
        return lax.dot_general(
            a, b, (((1,), (1 if transposed else 0,)), ((), ())),
            preferred_element_type=jnp.float32,
        )

    def times(both, top, columns, transposed):
        wide_part = dot(both, high[:, columns], transposed)
        count = top.shape[0]
        return wide_part[:count] + wide_part[count:] + dot(top, low[:, columns], transposed)

    groups = vecs // 8
    lane = lax.broadcasted_iota(jnp.int32, (8, width), 1)

    def send_sums(turn, values):
        packed = jnp.zeros((8, width), jnp.float32)
        for q, value in enumerate(values):
            for g in range(groups):
                packed = jnp.where(lane == q * groups + g, value[g * 8 : (g + 1) * 8], packed)
        sums_send[turn] = packed
        return [
            to_row(
                sums_send.at[turn],
                sums_recv.at[turn, peers - step],
                sums_sems.at[turn],
                step,
            )
            for step in range(1, n_rows)
        ]

    def total_sums(turn, copies, count):
        arrive(copies)
        total = sums_send[turn]
        for step in range(1, n_rows):
            total = total + sums_recv[turn, step - 1]
        return [
            jnp.concatenate(
                [total[:, q * groups + g : q * groups + g + 1] for g in range(groups)], axis=0
            )
            for q in range(count)
        ]

    def send_vectors(turn, vector):
        copies = []
        for step in range(1, n_rows):
            for slot in range(CAP):
                picked = jnp.zeros((vecs, width), jnp.float32)
                for row in range(block_rows):
                    piece = vector[:, row * width : (row + 1) * width]
                    picked = jnp.where(named(step, slot, row), piece, picked)
                vec_send[turn, step - 1, :, slot * width : (slot + 1) * width] = picked
            copies.append(
                to_row(
                    vec_send.at[turn, step - 1],
                    vec_recv.at[turn, peers - step],
                    vec_sems.at[turn],
                    step,
                )
            )
        return copies

    def apply_h(turn, vector, sums, later):
        if turn > 0:
            copies = send_vectors(turn, vector)
            sum_copies = send_sums(turn - 1, sums)
        top, bottom = split(vector)
        both = jnp.concatenate([top, bottom], axis=0)
        products = []
        for step in range(1, n_rows):
            columns = slice(mine + (step - 1) * pair, mine + step * pair)
            prod_send[turn, step - 1] = times(both, top, columns, False)
            products.append(
                to_row(
                    prod_send.at[turn, step - 1],
                    prod_recv.at[turn, peers - step],
                    prod_sems.at[turn],
                    step,
                )
            )
        if turn == 0:
            arrive(list_copies)
            copies = send_vectors(turn, vector)
            sum_copies = None
        if later is not None:
            col_copies.extend(later())
        near = slice(0, mine)
        result = times(both, top, near, False) + times(both, top, near, True)
        for step in range(1, n_rows):
            copies[peers - step].wait_recv()
            top, bottom = split(vec_recv[turn, step - 1])
            both = jnp.concatenate([top, bottom], axis=0)
            columns = slice(mine + (step - 1) * pair, mine + step * pair)
            result = result + times(both, top, columns, True)
        pieces = [result[:, row * width : (row + 1) * width] for row in range(block_rows)]
        for step in range(1, n_rows):
            products[peers - step].wait_recv()
            for slot in range(CAP):
                back = prod_recv[turn, step - 1, :, slot * width : (slot + 1) * width]
                for row in range(block_rows):
                    pieces[row] = pieces[row] + jnp.where(named(step, slot, row), back, 0.0)
        return jnp.concatenate(pieces, axis=1), sum_copies

    def column_sum(value):
        return jnp.sum(value, axis=1, keepdims=True)

    center = center_ref[0]
    poles = [shifts_ref[m] for m in range(shifts_ref.shape[0])]
    base = functools.reduce(jnp.minimum, poles)
    all_lanes = jnp.zeros((vecs, width), jnp.float32)

    col_copies = []

    def send_start():
        col_start[me_col] = vec_ref[...]
        return [
            to_col(vec_ref, col_start.at[me_col], col_sems.at[0], step)
            for step in range(1, n_cols)
        ]

    def send_residual():
        for row in range(block_rows):
            res_send[row] = residual[:, row * width : (row + 1) * width]
        col_res[me_col] = res_send[...]
        return [
            to_col(res_send, col_res.at[me_col], col_sems.at[1], step)
            for step in range(1, n_cols)
        ]

    start_image, _ = apply_h(0, start, None, send_start)
    half_one = start_image - center * start
    own_sums = [column_sum(start * start), column_sum(half_one * half_one)]
    second, sum_copies = apply_h(1, half_one, own_sums, None)
    start_norm, half_norm = total_sums(0, sum_copies, 2)
    alpha_one = start_norm / (half_norm + base * start_norm)
    op_image = second - center * half_one + base * start
    residual = start - alpha_one * op_image
    own_norm = column_sum(residual * residual)
    residual_image, sum_copies = apply_h(2, residual, [own_norm], send_residual)
    (res_norm,) = total_sums(1, sum_copies, 1)
    beta = res_norm / start_norm
    direction = residual + beta * start
    half_two = residual_image - center * residual + beta * half_one
    own_energy = column_sum(half_two * half_two + base * (direction * direction))
    (energy,) = total_sums(2, send_sums(2, [own_energy]), 1)
    alpha_one = alpha_one + all_lanes
    beta = beta + all_lanes
    alpha_two = res_norm / energy + all_lanes
    from_start = all_lanes
    from_residual = all_lanes
    for m, pole in enumerate(poles):
        delta = pole - base
        zeta_one = 1.0 / (1.0 + delta * alpha_one)
        zeta_two = (
            zeta_one
            * alpha_one
            / (
                alpha_two * beta * (1.0 - zeta_one)
                + alpha_one * (1.0 + delta * alpha_two)
            )
        )
        weight = weights_ref[m]
        from_start = from_start + weight * (
            alpha_one * zeta_one + alpha_two * beta * zeta_one * zeta_two
        )
        from_residual = from_residual + weight * (alpha_two * zeta_two)
    wide_lane = lax.broadcasted_iota(jnp.int32, (vecs, width), 1)
    factor_send[...] = jnp.where(wide_lane == 0, from_start, from_residual)
    factors[me_col] = factor_send[...]
    col_copies += [
        to_col(factor_send, factors.at[me_col], col_sems.at[2], step)
        for step in range(1, n_cols)
    ]
    along_start, along_res = from_start[:, 0:1], from_residual[:, 0:1]
    filtered = along_start * start + along_res * residual
    applied = along_start * start_image + along_res * residual_image
    for row in range(block_rows):
        out_ref[row] = filtered[:, row * width : (row + 1) * width]
    own = jnp.concatenate([filtered, applied], axis=0)
    arrive(col_copies)
    every = jnp.concatenate(
        [
            factors[c, :, 0:1] * flat(col_start.at[c]) + factors[c, :, 1:2] * flat(col_res.at[c])
            for c in range(n_cols)
        ],
        axis=0,
    )
    top, bottom = split(own)
    every_top, every_bottom = split(every)
    both = dot(jnp.concatenate([top, bottom], axis=0), every_top, True)
    count = 2 * vecs
    partial = both[:count] + both[count:] + dot(top, every_bottom, True)
    gram_send[...] = jnp.concatenate([partial[:vecs], partial[vecs:]], axis=1)
    gram_recv[me] = gram_send[...]
    gram_copies = [
        to_row(gram_send, gram_recv.at[me], gram_sems, step) for step in range(1, n_rows)
    ]
    arrive(gram_copies)
    summed = gram_recv[0]
    for device in range(1, n_rows):
        summed = summed + gram_recv[device]
    scaled = summed * (1.0 / (n_rows * mine))
    columns = n_cols * vecs
    gram_ref[...] = scaled[:, :columns]
    ritz_ref[...] = scaled[:, columns:]
    for copy in pending:
        copy.wait_send()


def fused_shards(
    n_rows, n_cols, hblocks, col_index, right_side, center, shifts, filter_weights
):
    block_rows, _, width, _ = hblocks.shape
    vecs = right_side.shape[1]
    peers = n_rows - 1
    spots = block_rows + CAP * peers
    mine = block_rows * width
    me = lax.axis_index("rows")
    high, low, lists = pack_blocks(n_rows, me.reshape(1), col_index, hblocks, spots)
    columns = n_cols * vecs
    pair = CAP * width
    vmem = pl.BlockSpec(memory_space=pltpu.VMEM)
    smem = pl.BlockSpec(memory_space=pltpu.SMEM)
    f32 = jnp.float32
    filtered, gram, ritz = pl.pallas_call(
        functools.partial(filter_kernel, n_rows, n_cols),
        out_shape=[
            jax.ShapeDtypeStruct(right_side.shape, f32),
            jax.ShapeDtypeStruct((vecs, columns), f32),
            jax.ShapeDtypeStruct((vecs, columns), f32),
        ],
        in_specs=[smem, smem, smem, vmem, vmem, vmem, vmem],
        out_specs=[vmem, vmem, vmem],
        scratch_shapes=[
            pltpu.VMEM((peers, CAP, width), f32),
            pltpu.VMEM((3, peers, vecs, pair), f32),
            pltpu.VMEM((3, peers, vecs, pair), f32),
            pltpu.VMEM((3, peers, vecs, pair), f32),
            pltpu.VMEM((3, peers, vecs, pair), f32),
            pltpu.VMEM((n_cols,) + right_side.shape, f32),
            pltpu.VMEM((n_cols,) + right_side.shape, f32),
            pltpu.VMEM(right_side.shape, f32),
            pltpu.VMEM((3, 8, width), f32),
            pltpu.VMEM((3, peers, 8, width), f32),
            pltpu.VMEM((vecs, width), f32),
            pltpu.VMEM((n_cols, vecs, width), f32),
            pltpu.VMEM((vecs, 2 * columns), f32),
            pltpu.VMEM((n_rows, vecs, 2 * columns), f32),
            pltpu.SemaphoreType.DMA((2, peers)),
            pltpu.SemaphoreType.DMA((3, 2, peers)),
            pltpu.SemaphoreType.DMA((3, 2, peers)),
            pltpu.SemaphoreType.DMA((3, 2, n_cols - 1)),
            pltpu.SemaphoreType.DMA((3, 2, peers)),
            pltpu.SemaphoreType.DMA((2, peers)),
        ],
        compiler_params=pltpu.CompilerParams(
            collective_id=0, has_side_effects=True, vmem_limit_bytes=24 << 20
        ),
    )(center, shifts, filter_weights, right_side, lists, high, low)
    return filtered, gram.T, ritz.T


def solution(mesh):
    placed = (P("rows", None, None, None), P("rows", None), P("rows", "cols", None), P(), P(), P())
    n_rows, n_cols = mesh.shape["rows"], mesh.shape["cols"]

    def body(hblocks, *rest):
        block_rows, per_row = hblocks.shape[:2]
        if CAP * (n_rows - 1) * block_rows <= block_rows * per_row:
            return fused_shards(n_rows, n_cols, hblocks, *rest)
        return shards(hblocks, *rest)

    return jax.shard_map(
        body,
        mesh=mesh,
        in_specs=placed,
        out_specs=(P("rows", "cols", None), P(None, "cols"), P(None, "cols")),
        check_vma=False,
    )
```
